256 devices in a mesh: op: 8 (over x, core), sec: 32 (over y, z).
Axes of the slice: x: 4, y: 4, z: 8, core: 2. Of those that a mesh axis runs over, the one named last changes fastest.
Arguments:
- wavefunction: bfloat16 [8192, 3, 4096], P('sec'), may hold values from -6 to 6
- left_ops: bfloat16 [8192, 24, 256], P('sec', 'op'), may hold values from -0.375 to 0.375
- right_ops: bfloat16 [24, 32, 128, 128], P('op', 'sec'), may hold values from -0.109375 to 0.109375
- term_shift: int32 [24], P('op'), may hold values from -1 to 1
Outputs:
- applied: bfloat16 [8192, 3, 4096], P('sec', None, 'op')
The draws below stay inside these ranges and needn't reach their ends.
All inputs are finite; a program needn't handle non-finite values.
Results may differ from the reference program's by a relative error of at most 0.017.
Values may be sent and summed in bfloat16 or wider, within the bound.
A program may use at most 128 MiB of HBM per device.

```python
import jax
import jax.numpy as jnp
from jax import lax

ML = 256
MR = 128
VECS = 3
K_DEV = 3
KTERMS = 24
LSECT = 32
RSECT = 32
NL = 8192
NR = 4096
N_OP = 8


def touch_ends(drawn, stream_key, smallest, largest):
    extent = drawn.shape
    place = [jax.random.randint(jax.random.fold_in(stream_key, axis), (), 0, extent[axis]) for axis in range(len(extent))]
    drawn = drawn.at[tuple(place)].set(smallest)
    longest = extent.index(max(extent))
    place[longest] = (place[longest] + 1) % extent[longest]
    return drawn.at[tuple(place)].set(largest)


def levels(stream_key, extent, split, smallest, largest):
    def one(dim, parts):
        steps = jax.random.uniform(jax.random.fold_in(jax.random.fold_in(stream_key, 6), dim), (parts,), jnp.float32, smallest / len(split), largest / len(split))
        return jnp.repeat(jnp.exp(steps), extent[dim] // parts).reshape((-1,) + (1,) * (len(extent) - dim - 1))

    gain = one(*split[0])
    for cut in split[1:]:
        gain = gain * one(*cut)
    return gain


def bell_draw(rng, dims, width, limit, cuts=(), held_as=jnp.bfloat16):
    values = width * jax.random.normal(rng, dims, jnp.float32)
    if cuts:
        values = values * levels(rng, dims, cuts, -0.22, 0.18)
    return jnp.clip(values, -limit, limit).astype(held_as)


def setup_inputs(seed: int = 0) -> dict:
    keys = jax.random.split(jax.random.key(seed), 5)
    return {
        "wavefunction": bell_draw(keys[0], (NL, VECS, NR), 1.0, 6.0, ((0, 32),)),
        "left_ops": bell_draw(keys[1], (NL, KTERMS, ML), ML ** -0.5, 0.375, ((0, 32), (1, 8))),
        "right_ops": bell_draw(keys[2], (KTERMS, RSECT, MR, MR), (MR * KTERMS) ** -0.5, 0.109375, ((0, 8), (1, 32))),
        "term_shift": touch_ends(jax.random.randint(keys[3], (KTERMS,), -1, 2), jax.random.fold_in(keys[3], 1), -1, 1).astype(jnp.int32),
    }


def reference(wavefunction, left_ops, right_ops, term_shift):
    blocks = wavefunction.astype(jnp.float32).reshape(LSECT, ML, VECS, NR)
    left_all = left_ops.astype(jnp.float32).reshape(LSECT, ML, KTERMS, ML)
    right_all = right_ops.astype(jnp.float32)
    sector_rows = jnp.arange(LSECT)
    sector_cols = jnp.arange(RSECT)
    applied = jnp.zeros((NL, VECS, NR), jnp.float32)
    for group in range(N_OP):
        partial_sum = jnp.zeros((NL, VECS, NR), jnp.float32)
        for inner in range(K_DEV):
            term = group * K_DEV + inner
            offset = term_shift[term]
            source = jnp.einsum("aij,ajvn->aivn", left_all[:, :, term, :], blocks).astype(jnp.bfloat16)
            source = lax.optimization_barrier(source)
            placed = jnp.roll(source, offset, axis=0)
            row_valid = (sector_rows - offset >= 0) & (sector_rows - offset < LSECT)
            placed = jnp.where(row_valid[:, None, None, None], placed, jnp.zeros((), jnp.bfloat16))
            columns = jnp.roll(placed.reshape(NL, VECS, RSECT, MR), -offset, axis=2)
            col_valid = (sector_cols + offset >= 0) & (sector_cols + offset < RSECT)
            result = jnp.einsum("nvbk,bkm->nvbm", columns.astype(jnp.float32), right_all[term])
            result = jnp.where(col_valid[None, None, :, None], result, jnp.zeros((), jnp.float32))
            partial_sum = partial_sum + result.reshape(NL, VECS, NR)
        rounded = lax.optimization_barrier(partial_sum.astype(jnp.bfloat16))
        applied = applied + rounded.astype(jnp.float32)
    return applied.astype(jnp.bfloat16)
```

```python
import functools

import jax
import jax.numpy as jnp
from jax import lax
from jax.experimental import pallas as pl
from jax.experimental.pallas import tpu as pltpu
from jax.sharding import PartitionSpec as P

X, CORES, Y, Z = 4, 2, 4, 8
GROUPS = X * CORES
SECTORS = Y * Z
OWN = SECTORS // GROUPS
MESH = pl.DeviceIdType.MESH


def kernel(
    w_hbm, l_hbm, r_hbm, sh_in, out,
    w, l, r, z, rm, acc, sbuf, rbuf, shv, shs,
    loc, ps, pr, zs, zr, ys, yr, ls, lr, ss, sr, os_, or_,
):
    op, sec = lax.axis_index("op"), lax.axis_index("sec")
    xx, core = lax.div(op, CORES), lax.rem(op, CORES)
    yy, zz = lax.div(sec, Z), lax.rem(sec, Z)
    vecs, ml, mr = w.shape[1], w.shape[2], w.shape[3]
    terms = l.shape[1]
    half = ml // 2

    def group(dx, other=0):
        return lax.rem(xx + dx + X, X) * CORES + (lax.rem(core + other, CORES))

    def z_of(d):
        return lax.rem(zz + d + Z, Z)

    def y_of(d):
        return lax.rem(yy + d + Y, Y)

    x_up, x_dn, sib = (group(1), sec), (group(-1), sec), (group(0, 1), sec)
    z_up, z_dn = (op, yy * Z + z_of(1)), (op, yy * Z + z_of(-1))
    y_up, y_dn = (op, y_of(1) * Z + zz), (op, y_of(-1) * Z + zz)
    s_up = (op, lax.rem(sec + 1, SECTORS))
    s_dn = (op, lax.rem(sec + SECTORS - 1, SECTORS))
    to_op, to_sec = lax.div(sec, OWN), xx * Z + lax.rem(sec, OWN) * CORES + core
    from_op = yy * CORES + lax.rem(zz, CORES)
    from_sec = op * OWN + lax.div(zz, CORES)
    stays = (to_op == op) & (to_sec == sec)
    moves = jnp.logical_not(stays)

    first = op * OWN - 1
    for k in range(OWN + 2):
        def load(k=k):
            at = pl.multiple_of((first + k) * mr, mr)
            pltpu.make_async_copy(w_hbm.at[:, :, pl.ds(at, mr)], w.at[k], loc.at[k]).start()

        def blank(k=k):
            w[k] = jnp.zeros(w.shape[1:], w.dtype)

        if k == 0:
            pl.when(op > 0)(load)
            pl.when(op == 0)(blank)
        elif k == OWN + 1:
            pl.when(op < GROUPS - 1)(load)
            pl.when(op == GROUPS - 1)(blank)
        else:
            load()
    own_l = pltpu.make_async_copy(l_hbm, l.at[op], loc.at[OWN + 2])
    own_l.start()
    own_sh = pltpu.make_async_copy(sh_in, shv.at[op], loc.at[OWN + 3])
    own_sh.start()

    barrier = pltpu.get_barrier_semaphore()
    greet = [z_up, z_dn, y_up, y_dn, s_up, s_dn]
    greet += [(lax.rem(op + d, GROUPS), sec) for d in range(1, GROUPS)]
    for who in greet:
        pl.semaphore_signal(barrier, inc=1, device_id=who, device_id_type=MESH)

    @pl.when(moves)
    def _():
        for who in ((to_op, to_sec), (from_op, from_sec)):
            pl.semaphore_signal(barrier, inc=1, device_id=who, device_id_type=MESH)
        pl.semaphore_wait(barrier, len(greet) + 2)

    @pl.when(stays)
    def _():
        pl.semaphore_wait(barrier, len(greet))

    sent = []

    def copy(src, dst, send, recv, who):
        return pltpu.make_async_remote_copy(
            src_ref=src, dst_ref=dst, send_sem=send, recv_sem=recv, device_id=who, device_id_type=MESH
        )

    def push(src, dst, send, recv, who):
        c = copy(src, dst, send, recv, who)
        c.start()
        sent.append(c)

    def got(dst, send, recv, who):
        copy(dst, dst, send, recv, who).wait_recv()

    @pl.when(moves)
    def _():
        copy(r_hbm, r.at[xx, lax.rem(sec, OWN) * CORES + core], ps.at[0], pr.at[0], (to_op, to_sec)).start()

    @pl.when(stays)
    def _():
        pltpu.make_async_copy(r_hbm, r.at[yy, zz], loc.at[OWN + 4]).start()

    for d in range(1, GROUPS):
        push(sh_in, shv.at[op], ss.at[d], sr.at[op], (lax.rem(op + d, GROUPS), sec))
    push(l_hbm, l.at[op], ls.at[2], lr.at[2], sib)
    push(l_hbm, l.at[op], ls.at[0], lr.at[0], x_up)
    push(l_hbm, l.at[op], ls.at[1], lr.at[1], x_dn)

    def row_send(c):
        blk = r.at[yy, c]
        push(blk, blk, ys.at[0, c], yr.at[0, c], y_up)
        push(blk, blk, ys.at[1, c], yr.at[1, c], y_dn)

    def row_forward(sigma):
        a, b = sigma * CORES, sigma * CORES + 1
        low, high = r.at[y_of(-1), a], r.at[y_of(1), b]
        got(low, ys.at[0, a], yr.at[0, a], y_dn)
        push(low, low, ys.at[2, a], yr.at[2, a], y_up)
        got(high, ys.at[1, b], yr.at[1, b], y_up)
        push(high, high, ys.at[2, b], yr.at[2, b], y_dn)

    def row_finish(sigma):
        a, b = sigma * CORES, sigma * CORES + 1
        got(r.at[y_of(1), a], ys.at[1, a], yr.at[1, a], y_up)
        got(r.at[y_of(-1), b], ys.at[0, b], yr.at[0, b], y_dn)
        got(r.at[y_of(2), a], ys.at[2, a], yr.at[2, a], y_dn)
        got(r.at[y_of(2), b], ys.at[2, b], yr.at[2, b], y_up)

    def hop_up(k):
        blk = r.at[yy, z_of(-k)]
        push(blk, blk, zs.at[k], zr.at[k], z_up)

    def hop_dn(k):
        blk = r.at[yy, z_of(k)]
        push(blk, blk, zs.at[4 + k], zr.at[4 + k], z_dn)

    def hop_got(k):
        got(r.at[yy, z_of(-k)], zs.at[k - 1], zr.at[k - 1], z_dn)
        if k < 4:
            got(r.at[yy, z_of(k)], zs.at[3 + k], zr.at[3 + k], z_up)

    def left_products(g):
        def one(i, carry):
            s = shs[g, 0, i]
            cols = jnp.concatenate(
                [w[s + 1 + b, v] for b in range(OWN) for v in range(vecs)], axis=1
            )
            prod = jnp.dot(l[g, i], cols, preferred_element_type=jnp.float32).astype(z.dtype)
            for b in range(OWN):
                for v in range(vecs):
                    n = b * vecs + v
                    z[b, v, g * terms + i] = prod[:, n * mr : (n + 1) * mr]
            return carry

        lax.fori_loop(0, terms, one, 0)

    def right_products(sigma):
        for g in range(GROUPS):
            for i in range(terms):
                s = shs[g, 0, i]
                blk = r[g // CORES, sigma * CORES + g % CORES, i]
                for q in range(3):
                    kept = jnp.where(jnp.full(blk.shape, s, jnp.int32) == q - 1, blk, jnp.zeros_like(blk))
                    rm[g * terms + i, :, q * mr : (q + 1) * mr] = kept

        def one(v, carry):
            lhs = jnp.concatenate([z[sigma, v, t] for t in range(GROUPS * terms)], axis=1)
            rhs = rm[...].reshape(GROUPS * terms * mr, 3 * mr)
            sums = jnp.dot(lhs, rhs, preferred_element_type=jnp.float32)
            sbuf[0, sigma, v] = sums[:, :mr].astype(sbuf.dtype)
            acc[sigma, v] = sums[:, mr : 2 * mr]
            sbuf[1, sigma, v] = sums[:, 2 * mr :].astype(sbuf.dtype)
            for q, who in ((0, s_dn), (1, s_up)):
                copy(sbuf.at[q, sigma, v], rbuf.at[q, sigma, v], os_.at[q, sigma, v], or_.at[q, sigma, v], who).start()
            return carry

        lax.fori_loop(0, vecs, one, 0)

    @pl.when(moves)
    def _():
        got(r.at[yy, zz], ps.at[0], pr.at[0], (from_op, from_sec))

    @pl.when(stays)
    def _():
        pltpu.make_async_copy(r_hbm, r.at[yy, zz], loc.at[OWN + 4]).wait()

    hop_up(0)
    hop_dn(0)
    row_send(zz)

    turn = 1 - 2 * lax.rem(zz, 2)
    s0 = lax.div(zz, CORES)
    order = [s0, lax.rem(s0 - turn + OWN, OWN), lax.rem(s0 + turn + OWN, OWN), lax.rem(s0 + 2, OWN)]

    own_sh.wait()
    for d in range(1, GROUPS):
        g = lax.rem(op + d, GROUPS)
        got(shv.at[g], ss.at[GROUPS - d], sr.at[g], (g, sec))
    shift_in = pltpu.make_async_copy(shv, shs, loc.at[OWN + 5])
    shift_in.start()
    shift_in.wait()
    own_l.wait()
    for k in range(OWN + 2):
        def arrived(k=k):
            pltpu.make_async_copy(w_hbm.at[:, :, pl.ds(0, mr)], w.at[k], loc.at[k]).wait()

        if k == 0:
            pl.when(op > 0)(arrived)
        elif k == OWN + 1:
            pl.when(op < GROUPS - 1)(arrived)
        else:
            arrived()
    left_products(op)

    hop_got(1)
    hop_up(1)
    hop_dn(1)
    row_send(z_of(turn))

    got(l.at[group(0, 1)], ls.at[2], lr.at[2], sib)
    left_products(group(0, 1))

    g_dn, g_up, g_far = group(-1), group(1), group(2)
    got(l.at[g_dn], ls.at[0], lr.at[0], x_dn)
    push(l.at[g_dn, :, :half], l.at[g_dn, :, :half], ls.at[5], lr.at[5], x_up)
    push(l.at[g_dn], l.at[g_dn], ls.at[3], lr.at[3], sib)
    got(l.at[g_up], ls.at[1], lr.at[1], x_up)
    push(l.at[g_up, :, half:], l.at[g_up, :, half:], ls.at[6], lr.at[6], x_dn)
    push(l.at[g_up], l.at[g_up], ls.at[4], lr.at[4], sib)

    hop_got(2)
    hop_up(2)
    hop_dn(2)
    row_send(order[1] * CORES)
    row_send(order[1] * CORES + 1)
    row_forward(order[0])

    left_products(g_dn)
    left_products(g_up)

    hop_got(3)
    hop_up(3)
    row_send(order[2] * CORES)
    row_send(order[2] * CORES + 1)
    row_forward(order[1])

    got(l.at[g_far, :, :half], ls.at[5], lr.at[5], x_dn)
    push(l.at[g_far, :, :half], l.at[g_far, :, :half], ls.at[7], lr.at[7], sib)
    got(l.at[g_far, :, half:], ls.at[6], lr.at[6], x_up)
    push(l.at[g_far, :, half:], l.at[g_far, :, half:], ls.at[8], lr.at[8], sib)
    got(l.at[group(-1, 1)], ls.at[3], lr.at[3], sib)
    left_products(group(-1, 1))
    got(l.at[group(1, 1)], ls.at[4], lr.at[4], sib)
    left_products(group(1, 1))

    hop_got(4)
    row_send(order[3] * CORES)
    row_send(order[3] * CORES + 1)
    row_forward(order[2])

    left_products(g_far)
    got(l.at[group(2, 1), :, :half], ls.at[7], lr.at[7], sib)
    got(l.at[group(2, 1), :, half:], ls.at[8], lr.at[8], sib)
    left_products(group(2, 1))

    row_finish(order[0])
    right_products(order[0])
    row_forward(order[3])
    for sigma in order[1:]:
        row_finish(sigma)
        right_products(sigma)

    def total(sigma, carry):
        for v in range(vecs):
            got(rbuf.at[0, sigma, v], os_.at[0, sigma, v], or_.at[0, sigma, v], s_up)
            got(rbuf.at[1, sigma, v], os_.at[1, sigma, v], or_.at[1, sigma, v], s_dn)
        for v in range(vecs):
            above = rbuf[0, sigma, v].astype(jnp.float32)
            below = rbuf[1, sigma, v].astype(jnp.float32)
            whole = acc[sigma, v]
            whole = whole + jnp.where(jnp.full(above.shape, sec, jnp.int32) < SECTORS - 1, above, 0.0)
            whole = whole + jnp.where(jnp.full(below.shape, sec, jnp.int32) > 0, below, 0.0)
            at = pl.multiple_of(sigma * mr, mr)
            out[v, :, pl.ds(at, mr)] = whole.astype(out.dtype)
        return carry

    lax.fori_loop(0, OWN, total, 0)

    for c in sent:
        c.wait_send()

    @pl.when(moves)
    def _():
        copy(r_hbm, r.at[xx, lax.rem(sec, OWN) * CORES + core], ps.at[0], pr.at[0], (to_op, to_sec)).wait_send()

    def drain(sigma, carry):
        for v in range(vecs):
            for q, who in ((0, s_dn), (1, s_up)):
                copy(
                    sbuf.at[q, sigma, v], rbuf.at[q, sigma, v], os_.at[q, sigma, v], or_.at[q, sigma, v], who
                ).wait_send()
        return carry

    lax.fori_loop(0, OWN, drain, 0)


def on_device(wavefunction, left_ops, right_ops, term_shift):
    ml, vecs, _ = wavefunction.shape
    terms, mr = left_ops.shape[1], right_ops.shape[2]
    shifts = jnp.pad(term_shift.reshape(1, terms), ((0, 7), (0, 128 - terms)))
    every = GROUPS * terms
    flops = 2 * every * ml * ml * vecs * OWN * mr + 2 * every * vecs * ml * mr * OWN * mr
    anywhere = pl.BlockSpec(memory_space=pl.ANY)
    dma = pltpu.SemaphoreType.DMA
    bf16 = wavefunction.dtype
    result = pl.pallas_call(
        kernel,
        out_shape=jax.ShapeDtypeStruct((vecs, ml, OWN * mr), bf16),
        in_specs=[anywhere, anywhere, anywhere, anywhere],
        out_specs=pl.BlockSpec(memory_space=pltpu.VMEM),
        scratch_shapes=[
            pltpu.VMEM((OWN + 2, vecs, ml, mr), bf16),
            pltpu.VMEM((GROUPS, terms, ml, ml), bf16),
            pltpu.VMEM((Y, Z, terms, mr, mr), bf16),
            pltpu.VMEM((OWN, vecs, every, ml, mr), bf16),
            pltpu.VMEM((every, mr, 3 * mr), bf16),
            pltpu.VMEM((OWN, vecs, ml, mr), jnp.float32),
            pltpu.VMEM((2, OWN, vecs, ml, mr), bf16),
            pltpu.VMEM((2, OWN, vecs, ml, mr), bf16),
            pltpu.VMEM((GROUPS, 8, 128), jnp.int32),
            pltpu.SMEM((GROUPS, 8, 128), jnp.int32),
            dma((OWN + 6,)),
            dma((1,)), dma((1,)),
            dma((7,)), dma((7,)),
            dma((3, Z)), dma((3, Z)),
            dma((9,)), dma((9,)),
            dma((GROUPS,)), dma((GROUPS,)),
            dma((2, OWN, vecs)), dma((2, OWN, vecs)),
        ],
        compiler_params=pltpu.CompilerParams(
            collective_id=0, has_side_effects=True, vmem_limit_bytes=56 * 2**20
        ),
        cost_estimate=pl.CostEstimate(flops=flops, bytes_accessed=4 * 2**20, transcendentals=0),
    )(
        jnp.transpose(wavefunction, (1, 0, 2)),
        jnp.transpose(left_ops, (1, 0, 2)),
        right_ops.reshape(terms, mr, mr),
        shifts,
    )
    return jnp.transpose(result, (1, 0, 2))


def solution(mesh):
    in_specs = (P("sec", None, None), P("sec", "op", None), P("op", "sec", None, None), P("op"))
    out_specs = P("sec", None, "op")
    return jax.shard_map(
        on_device, mesh=mesh, in_specs=in_specs, out_specs=out_specs, check_vma=False
    )
```

```python
import functools

import jax
import jax.numpy as jnp
from jax import lax
from jax.experimental import pallas as pl
from jax.experimental.pallas import tpu as pltpu
from jax.sharding import PartitionSpec as P

X, CORES, Y, Z = 4, 2, 4, 8
GROUPS = X * CORES
SECTORS = Y * Z
OWN = SECTORS // GROUPS
MESH = pl.DeviceIdType.MESH


def kernel(
    w_hbm, l_hbm, r_hbm, sh_in, out,
    w, l, r, z, rm, acc, sbuf, rbuf, shv, shs,
    loc, ps, pr, zs, zr, ys, yr, ls, lr, ss, sr, os_, or_,
):
    op, sec = lax.axis_index("op"), lax.axis_index("sec")
    xx, core = lax.div(op, CORES), lax.rem(op, CORES)
    yy, zz = lax.div(sec, Z), lax.rem(sec, Z)
    vecs, ml, mr = w.shape[1], w.shape[2], w.shape[3]
    terms = l.shape[1]
    half = ml // 2

    def group(dx, other=0):
        return lax.rem(xx + dx + X, X) * CORES + (lax.rem(core + other, CORES))

    def z_of(d):
        return lax.rem(zz + d + Z, Z)

    def y_of(d):
        return lax.rem(yy + d + Y, Y)

    x_up, x_dn, sib = (group(1), sec), (group(-1), sec), (group(0, 1), sec)
    z_up, z_dn = (op, yy * Z + z_of(1)), (op, yy * Z + z_of(-1))
    y_up, y_dn = (op, y_of(1) * Z + zz), (op, y_of(-1) * Z + zz)
    s_up = (op, lax.rem(sec + 1, SECTORS))
    s_dn = (op, lax.rem(sec + SECTORS - 1, SECTORS))
    def pair_of(n, c):
        return lax.rem(n + OWN - 1 + 2 * c, OWN)

    def sector_of(p):
        return lax.rem(p + 1 + 2 * core, OWN)

    def far_y(d):
        return lax.rem(d + 2, Y)

    to_op = lax.div(sec, OWN)
    to_y, to_z = far_y(xx), pair_of(lax.rem(sec, OWN), lax.rem(to_op, CORES)) * CORES + core
    to_sec = to_y * Z + to_z
    from_op = far_y(yy) * CORES + lax.rem(zz, CORES)
    from_sec = op * OWN + sector_of(lax.div(zz, CORES))
    stays = (to_op == op) & (to_sec == sec)
    moves = jnp.logical_not(stays)

    first = op * OWN - 1
    for k in range(OWN + 2):
        def load(k=k):
            at = pl.multiple_of((first + k) * mr, mr)
            pltpu.make_async_copy(w_hbm.at[:, :, pl.ds(at, mr)], w.at[k], loc.at[k]).start()

        def blank(k=k):
            w[k] = jnp.zeros(w.shape[1:], w.dtype)

        if k == 0:
            pl.when(op > 0)(load)
            pl.when(op == 0)(blank)
        elif k == OWN + 1:
            pl.when(op < GROUPS - 1)(load)
            pl.when(op == GROUPS - 1)(blank)
        else:
            load()
    own_l = pltpu.make_async_copy(l_hbm, l.at[op], loc.at[OWN + 2])
    own_l.start()
    lane = lax.broadcasted_iota(jnp.int32, shv.shape[1:], 1)
    own_shifts = jnp.zeros(shv.shape[1:], jnp.int32)
    for i in range(terms):
        own_shifts = jnp.where(lane == i, jnp.full(lane.shape, sh_in[i], jnp.int32), own_shifts)
    shv[op] = own_shifts

    barrier = pltpu.get_barrier_semaphore()
    greet = [z_up, z_dn, y_up, y_dn, s_up, s_dn]
    greet += [(lax.rem(op + d, GROUPS), sec) for d in range(1, GROUPS)]
    for who in greet:
        pl.semaphore_signal(barrier, inc=1, device_id=who, device_id_type=MESH)

    @pl.when(moves)
    def _():
        for who in ((to_op, to_sec), (from_op, from_sec)):
            pl.semaphore_signal(barrier, inc=1, device_id=who, device_id_type=MESH)
        pl.semaphore_wait(barrier, len(greet) + 2)

    @pl.when(stays)
    def _():
        pl.semaphore_wait(barrier, len(greet))

    sent = []

    def copy(src, dst, send, recv, who):
        return pltpu.make_async_remote_copy(
            src_ref=src, dst_ref=dst, send_sem=send, recv_sem=recv, device_id=who, device_id_type=MESH
        )

    def push(src, dst, send, recv, who):
        c = copy(src, dst, send, recv, who)
        c.start()
        sent.append(c)

    def got(dst, send, recv, who):
        copy(dst, dst, send, recv, who).wait_recv()

    @pl.when(moves)
    def _():
        for i in range(terms):
            copy(r_hbm.at[i], r.at[to_y, to_z, i], ps.at[i], pr.at[i], (to_op, to_sec)).start()

    @pl.when(stays)
    def _():
        pltpu.make_async_copy(r_hbm, r.at[yy, zz], loc.at[OWN + 4]).start()

    for d in range(1, GROUPS):
        push(shv.at[op], shv.at[op], ss.at[d], sr.at[op], (lax.rem(op + d, GROUPS), sec))
    push(l_hbm, l.at[op], ls.at[2], lr.at[2], sib)
    push(l_hbm, l.at[op], ls.at[0], lr.at[0], x_up)
    push(l_hbm, l.at[op], ls.at[1], lr.at[1], x_dn)

    def row_send(c):
        blk = r.at[yy, c]
        push(blk, blk, ys.at[0, c], yr.at[0, c], y_up)
        push(blk, blk, ys.at[1, c], yr.at[1, c], y_dn)

    def passage(c):
        if c:
            upward = jnp.where(zz == Z - 1, 1, 0)
        else:
            upward = jnp.where(zz == 0, 0, 1)
        to = (op, y_of(2 * upward - 1) * Z + zz)
        source = (op, y_of(1 - 2 * upward) * Z + zz)
        return 1 - upward, to, source

    def row_forward(p):
        for c in range(CORES):
            at = p * CORES + c
            way, to, source = passage(c)
            blk = r.at[y_of(2 * way - 1), at]
            got(blk, ys.at[way, at], yr.at[way, at], source)
            push(blk, blk, ys.at[2, at], yr.at[2, at], to)

    def row_finish(p):
        for c in range(CORES):
            at = p * CORES + c
            way, to, source = passage(c)
            got(r.at[y_of(1 - 2 * way), at], ys.at[1 - way, at], yr.at[1 - way, at], to)
            got(r.at[y_of(2), at], ys.at[2, at], yr.at[2, at], source)

    def hop_up(k, i):
        blk = r.at[yy, z_of(-k), i]
        push(blk, blk, zs.at[k, i], zr.at[k, i], z_up)

    def hop_dn(k, i):
        blk = r.at[yy, z_of(k), i]
        push(blk, blk, zs.at[4 + k, i], zr.at[4 + k, i], z_dn)

    def hop(k):
        for i in range(terms):
            got(r.at[yy, z_of(-k), i], zs.at[k - 1, i], zr.at[k - 1, i], z_dn)
            if k < 4:
                hop_up(k, i)
                got(r.at[yy, z_of(k), i], zs.at[3 + k, i], zr.at[3 + k, i], z_up)
            if k < 3:
                hop_dn(k, i)

    def left_products(g):
        def one(i, carry):
            s = shs[g, 0, i]
            cols = jnp.concatenate(
                [w[s + 1 + b, v] for b in range(OWN) for v in range(vecs)], axis=1
            )
            prod = jnp.dot(l[g, i], cols, preferred_element_type=jnp.float32).astype(z.dtype)
            for b in range(OWN):
                for v in range(vecs):
                    n = b * vecs + v
                    z[b, v, g * terms + i] = prod[:, n * mr : (n + 1) * mr]
            return carry

        lax.fori_loop(0, terms, one, 0)

    def right_products(p):
        sigma = sector_of(p)
        for g in range(GROUPS):
            for i in range(terms):
                s = shs[g, 0, i]
                blk = r[(g // CORES + 2) % Y, p * CORES + g % CORES, i]
                for q in range(3):
                    kept = jnp.where(jnp.full(blk.shape, s, jnp.int32) == q - 1, blk, jnp.zeros_like(blk))
                    rm[g * terms + i, :, q * mr : (q + 1) * mr] = kept

        def one(v, carry):
            lhs = jnp.concatenate([z[sigma, v, t] for t in range(GROUPS * terms)], axis=1)
            rhs = rm[...].reshape(GROUPS * terms * mr, 3 * mr)
            sums = jnp.dot(lhs, rhs, preferred_element_type=jnp.float32)
            sbuf[0, sigma, v] = sums[:, :mr].astype(sbuf.dtype)
            acc[sigma, v] = sums[:, mr : 2 * mr]
            sbuf[1, sigma, v] = sums[:, 2 * mr :].astype(sbuf.dtype)
            for q, who in ((0, s_dn), (1, s_up)):
                copy(sbuf.at[q, sigma, v], rbuf.at[q, sigma, v], os_.at[q, sigma, v], or_.at[q, sigma, v], who).start()
            return carry

        lax.fori_loop(0, vecs, one, 0)

    @pl.when(stays)
    def _():
        pltpu.make_async_copy(r_hbm, r.at[yy, zz], loc.at[OWN + 4]).wait()

    for i in range(terms):
        @pl.when(moves)
        def _(i=i):
            got(r.at[yy, zz, i], ps.at[i], pr.at[i], (from_op, from_sec))

        hop_up(0, i)
        hop_dn(0, i)
    row_send(zz)

    turn = 1 - 2 * lax.rem(zz, 2)
    s0 = lax.div(zz, CORES)
    order = [s0, lax.rem(s0 - turn + OWN, OWN), lax.rem(s0 + turn + OWN, OWN), lax.rem(s0 + 2, OWN)]

    for d in range(1, GROUPS):
        g = lax.rem(op + d, GROUPS)
        got(shv.at[g], ss.at[GROUPS - d], sr.at[g], (g, sec))
    shift_in = pltpu.make_async_copy(shv, shs, loc.at[OWN + 5])
    shift_in.start()
    shift_in.wait()
    own_l.wait()
    for k in range(OWN + 2):
        def arrived(k=k):
            pltpu.make_async_copy(w_hbm.at[:, :, pl.ds(0, mr)], w.at[k], loc.at[k]).wait()

        if k == 0:
            pl.when(op > 0)(arrived)
        elif k == OWN + 1:
            pl.when(op < GROUPS - 1)(arrived)
        else:
            arrived()
    left_products(op)

    hop(1)
    row_send(z_of(turn))

    got(l.at[group(0, 1)], ls.at[2], lr.at[2], sib)
    left_products(group(0, 1))

    g_dn, g_up, g_far = group(-1), group(1), group(2)
    got(l.at[g_dn], ls.at[0], lr.at[0], x_dn)
    push(l.at[g_dn, :, :half], l.at[g_dn, :, :half], ls.at[5], lr.at[5], x_up)
    push(l.at[g_dn], l.at[g_dn], ls.at[3], lr.at[3], sib)
    got(l.at[g_up], ls.at[1], lr.at[1], x_up)
    push(l.at[g_up, :, half:], l.at[g_up, :, half:], ls.at[6], lr.at[6], x_dn)
    push(l.at[g_up], l.at[g_up], ls.at[4], lr.at[4], sib)

    hop(2)
    row_send(order[1] * CORES)
    row_send(order[1] * CORES + 1)
    row_forward(order[0])

    left_products(g_dn)
    left_products(g_up)

    hop(3)
    row_send(order[2] * CORES)
    row_send(order[2] * CORES + 1)
    row_forward(order[1])

    got(l.at[g_far, :, :half], ls.at[5], lr.at[5], x_dn)
    push(l.at[g_far, :, :half], l.at[g_far, :, :half], ls.at[7], lr.at[7], sib)
    got(l.at[g_far, :, half:], ls.at[6], lr.at[6], x_up)
    push(l.at[g_far, :, half:], l.at[g_far, :, half:], ls.at[8], lr.at[8], sib)
    got(l.at[group(-1, 1)], ls.at[3], lr.at[3], sib)
    left_products(group(-1, 1))
    got(l.at[group(1, 1)], ls.at[4], lr.at[4], sib)
    left_products(group(1, 1))

    hop(4)
    row_send(order[3] * CORES)
    row_send(order[3] * CORES + 1)
    row_forward(order[2])

    left_products(g_far)
    got(l.at[group(2, 1), :, :half], ls.at[7], lr.at[7], sib)
    got(l.at[group(2, 1), :, half:], ls.at[8], lr.at[8], sib)
    left_products(group(2, 1))

    row_finish(order[0])
    right_products(order[0])
    row_forward(order[3])
    for p in order[1:]:
        row_finish(p)
        right_products(p)

    def total(sigma, carry):
        for v in range(vecs):
            got(rbuf.at[0, sigma, v], os_.at[0, sigma, v], or_.at[0, sigma, v], s_up)
            got(rbuf.at[1, sigma, v], os_.at[1, sigma, v], or_.at[1, sigma, v], s_dn)
        for v in range(vecs):
            above = rbuf[0, sigma, v].astype(jnp.float32)
            below = rbuf[1, sigma, v].astype(jnp.float32)
            whole = acc[sigma, v]
            whole = whole + jnp.where(jnp.full(above.shape, sec, jnp.int32) < SECTORS - 1, above, 0.0)
            whole = whole + jnp.where(jnp.full(below.shape, sec, jnp.int32) > 0, below, 0.0)
            at = pl.multiple_of(sigma * mr, mr)
            out[v, :, pl.ds(at, mr)] = whole.astype(out.dtype)
        return carry

    lax.fori_loop(0, OWN, total, 0)

    for c in sent:
        c.wait_send()

    @pl.when(moves)
    def _():
        for i in range(terms):
            copy(r_hbm.at[i], r.at[to_y, to_z, i], ps.at[i], pr.at[i], (to_op, to_sec)).wait_send()

    def drain(sigma, carry):
        for v in range(vecs):
            for q, who in ((0, s_dn), (1, s_up)):
                copy(
                    sbuf.at[q, sigma, v], rbuf.at[q, sigma, v], os_.at[q, sigma, v], or_.at[q, sigma, v], who
                ).wait_send()
        return carry

    lax.fori_loop(0, OWN, drain, 0)


def on_device(wavefunction, left_ops, right_ops, term_shift):
    ml, vecs, _ = wavefunction.shape
    terms, mr = left_ops.shape[1], right_ops.shape[2]
    every = GROUPS * terms
    flops = 2 * every * ml * ml * vecs * OWN * mr + 2 * every * vecs * ml * mr * OWN * mr
    anywhere = pl.BlockSpec(memory_space=pl.ANY)
    dma = pltpu.SemaphoreType.DMA
    bf16 = wavefunction.dtype
    result = pl.pallas_call(
        kernel,
        out_shape=jax.ShapeDtypeStruct((vecs, ml, OWN * mr), bf16),
        in_specs=[anywhere, anywhere, anywhere, pl.BlockSpec(memory_space=pltpu.SMEM)],
        out_specs=pl.BlockSpec(memory_space=pltpu.VMEM),
        scratch_shapes=[
            pltpu.VMEM((OWN + 2, vecs, ml, mr), bf16),
            pltpu.VMEM((GROUPS, terms, ml, ml), bf16),
            pltpu.VMEM((Y, Z, terms, mr, mr), bf16),
            pltpu.VMEM((OWN, vecs, every, ml, mr), bf16),
            pltpu.VMEM((every, mr, 3 * mr), bf16),
            pltpu.VMEM((OWN, vecs, ml, mr), jnp.float32),
            pltpu.VMEM((2, OWN, vecs, ml, mr), bf16),
            pltpu.VMEM((2, OWN, vecs, ml, mr), bf16),
            pltpu.VMEM((GROUPS, 8, 128), jnp.int32),
            pltpu.SMEM((GROUPS, 8, 128), jnp.int32),
            dma((OWN + 6,)),
            dma((terms,)), dma((terms,)),
            dma((7, terms)), dma((7, terms)),
            dma((3, Z)), dma((3, Z)),
            dma((9,)), dma((9,)),
            dma((GROUPS,)), dma((GROUPS,)),
            dma((2, OWN, vecs)), dma((2, OWN, vecs)),
        ],
        compiler_params=pltpu.CompilerParams(
            collective_id=0, has_side_effects=True, vmem_limit_bytes=56 * 2**20
        ),
        cost_estimate=pl.CostEstimate(flops=flops, bytes_accessed=4 * 2**20, transcendentals=0),
    )(
        jnp.transpose(wavefunction, (1, 0, 2)),
        jnp.transpose(left_ops, (1, 0, 2)),
        right_ops.reshape(terms, mr, mr),
        term_shift,
    )
    return jnp.transpose(result, (1, 0, 2))


def solution(mesh):
    in_specs = (P("sec", None, None), P("sec", "op", None), P("op", "sec", None, None), P("op"))
    out_specs = P("sec", None, "op")
    return jax.shard_map(
        on_device, mesh=mesh, in_specs=in_specs, out_specs=out_specs, check_vma=False
    )
```

```python
import jax
import jax.numpy as jnp
from jax import lax
from jax.experimental import pallas as pl
from jax.experimental.pallas import tpu as pltpu
from jax.sharding import PartitionSpec as P

X, CORES, Y, Z = 4, 2, 4, 8
GROUPS = X * CORES
SECTORS = Y * Z
OWN = SECTORS // GROUPS
EVEN = 1
MESH = pl.DeviceIdType.MESH


def kernel(
    w_hbm, l_hbm, r_hbm, sh_in, out,
    w, l, r, z, rs, near, acc, sbuf, rbuf, shv, shs,
    loc, ps, pr, zs, zr, ys, yr, ls, lr, ss, sr, os_, or_,
):
    op, sec = lax.axis_index("op"), lax.axis_index("sec")
    xx, core = lax.div(op, CORES), lax.rem(op, CORES)
    yy, zz = lax.div(sec, Z), lax.rem(sec, Z)
    vecs, ml, mr = w.shape[1], w.shape[2], w.shape[3]
    terms = l.shape[1]
    half = ml // 2

    def group(dx, other=0):
        return lax.rem(xx + dx + X, X) * CORES + (lax.rem(core + other, CORES))

    def z_of(d):
        return lax.rem(zz + d + Z, Z)

    def y_of(d):
        return lax.rem(yy + d + Y, Y)

    x_up, x_dn, sib = (group(1), sec), (group(-1), sec), (group(0, 1), sec)
    z_up, z_dn = (op, yy * Z + z_of(1)), (op, yy * Z + z_of(-1))
    y_up, y_dn = (op, y_of(1) * Z + zz), (op, y_of(-1) * Z + zz)
    s_up = (op, lax.rem(sec + 1, SECTORS))
    s_dn = (op, lax.rem(sec + SECTORS - 1, SECTORS))
    def pair_of(n, c):
        return lax.rem(n + OWN - 1 + 2 * c, OWN)

    def sector_of(p):
        return lax.rem(p + 1 + 2 * core, OWN)

    def far_y(d):
        return lax.rem(d + 2, Y)

    to_op = lax.div(sec, OWN)
    to_y, to_z = far_y(xx), pair_of(lax.rem(sec, OWN), lax.rem(to_op, CORES)) * CORES + core
    to_sec = to_y * Z + to_z
    from_op = far_y(yy) * CORES + lax.rem(zz, CORES)
    from_sec = op * OWN + sector_of(lax.div(zz, CORES))
    stays = (to_op == op) & (to_sec == sec)
    moves = jnp.logical_not(stays)

    first = op * OWN - 1
    for k in range(OWN + 2):
        def load(k=k):
            at = pl.multiple_of((first + k) * mr, mr)
            pltpu.make_async_copy(w_hbm.at[:, :, pl.ds(at, mr)], w.at[k], loc.at[k]).start()

        def blank(k=k):
            w[k] = jnp.zeros(w.shape[1:], w.dtype)

        if k == 0:
            pl.when(op > 0)(load)
            pl.when(op == 0)(blank)
        elif k == OWN + 1:
            pl.when(op < GROUPS - 1)(load)
            pl.when(op == GROUPS - 1)(blank)
        else:
            load()
    own_l = pltpu.make_async_copy(l_hbm, l.at[op], loc.at[OWN + 2])
    own_l.start()
    lane = lax.broadcasted_iota(jnp.int32, shv.shape[1:], 1)
    own_shifts = jnp.zeros(shv.shape[1:], jnp.int32)
    for i in range(terms):
        own_shifts = jnp.where(lane == i, jnp.full(lane.shape, sh_in[i], jnp.int32), own_shifts)
    shv[op] = own_shifts

    barrier = pltpu.get_barrier_semaphore()
    greet = [z_up, z_dn, y_up, y_dn, s_up, s_dn]
    greet += [(lax.rem(op + d, GROUPS), sec) for d in range(1, GROUPS)]
    for who in greet:
        pl.semaphore_signal(barrier, inc=1, device_id=who, device_id_type=MESH)

    @pl.when(moves)
    def _():
        for who in ((to_op, to_sec), (from_op, from_sec)):
            pl.semaphore_signal(barrier, inc=1, device_id=who, device_id_type=MESH)
        pl.semaphore_wait(barrier, len(greet) + 2)

    @pl.when(stays)
    def _():
        pl.semaphore_wait(barrier, len(greet))

    turn = 1 - 2 * lax.rem(zz, 2)
    s0 = lax.div(zz, CORES)
    order = [s0, lax.rem(s0 - turn + OWN, OWN), lax.rem(s0 + turn + OWN, OWN), lax.rem(s0 + 2, OWN)]

    sent = []

    def copy(src, dst, send, recv, who):
        return pltpu.make_async_remote_copy(
            src_ref=src, dst_ref=dst, send_sem=send, recv_sem=recv, device_id=who, device_id_type=MESH
        )

    def push(src, dst, send, recv, who):
        c = copy(src, dst, send, recv, who)
        c.start()
        sent.append(c)

    def got(dst, send, recv, who):
        copy(dst, dst, send, recv, who).wait_recv()

    @pl.when(moves)
    def _():
        for i in range(terms):
            copy(r_hbm.at[i], r.at[to_y, to_z, i], ps.at[i], pr.at[i], (to_op, to_sec)).start()

    @pl.when(stays)
    def _():
        pltpu.make_async_copy(r_hbm, r.at[yy, zz], loc.at[OWN + 4]).start()

    for d in range(1, GROUPS):
        push(shv.at[op], shv.at[op], ss.at[d], sr.at[op], (lax.rem(op + d, GROUPS), sec))
    for i in range(terms):
        push(l_hbm.at[i], l.at[op, i], ls.at[0, i], lr.at[0, i], x_up)
        push(l_hbm.at[i], l.at[op, i], ls.at[1, i], lr.at[1, i], x_dn)
        push(l_hbm.at[i], l.at[op, i], ls.at[2, i], lr.at[2, i], sib)
    g_dn, g_up, g_far = group(-1), group(1), group(2)

    def left_near(i):
        blk, part = l.at[g_dn, i], l.at[g_dn, i, :half]
        got(blk, ls.at[0, i], lr.at[0, i], x_dn)
        push(part, part, ls.at[5, i], lr.at[5, i], x_up)
        push(blk, blk, ls.at[3, i], lr.at[3, i], sib)
        blk, part = l.at[g_up, i], l.at[g_up, i, half:]
        got(blk, ls.at[1, i], lr.at[1, i], x_up)
        push(part, part, ls.at[6, i], lr.at[6, i], x_dn)
        push(blk, blk, ls.at[4, i], lr.at[4, i], sib)

    def left_far(i):
        part = l.at[g_far, i, :half]
        got(part, ls.at[5, i], lr.at[5, i], x_dn)
        push(part, part, ls.at[7, i], lr.at[7, i], sib)
        part = l.at[g_far, i, half:]
        got(part, ls.at[6, i], lr.at[6, i], x_up)
        push(part, part, ls.at[8, i], lr.at[8, i], sib)

    def left_sibling(dx, *ways):
        for i in range(terms):
            for way in ways:
                blk = l.at[group(dx, 1), i]
                if len(ways) > 1:
                    blk = l.at[group(dx, 1), i, :half] if way == ways[0] else l.at[group(dx, 1), i, half:]
                got(blk, ls.at[way, i], lr.at[way, i], sib)

    def row_send(c):
        blk = r.at[yy, c]
        push(blk, blk, ys.at[0, c], yr.at[0, c], y_up)
        push(blk, blk, ys.at[1, c], yr.at[1, c], y_dn)

    def passage(c, p):
        late = sum((p == order[k]).astype(jnp.int32) for k in range(EVEN, OWN)) > 0
        if c:
            upward = jnp.where((zz == Z - 1) & late, 1, 0)
        else:
            upward = jnp.where((zz == 0) & late, 0, 1)
        to = (op, y_of(2 * upward - 1) * Z + zz)
        source = (op, y_of(1 - 2 * upward) * Z + zz)
        return 1 - upward, to, source

    def row_forward(p):
        for c in range(CORES):
            at = p * CORES + c
            way, to, source = passage(c, p)
            blk = r.at[y_of(2 * way - 1), at]
            got(blk, ys.at[way, at], yr.at[way, at], source)
            push(blk, blk, ys.at[2, at], yr.at[2, at], to)

    def row_near(p):
        for c in range(CORES):
            at = p * CORES + c
            way, to, _ = passage(c, p)
            got(r.at[y_of(1 - 2 * way), at], ys.at[1 - way, at], yr.at[1 - way, at], to)

    def row_far(p):
        for c in range(CORES):
            at = p * CORES + c
            _, _, source = passage(c, p)
            got(r.at[y_of(2), at], ys.at[2, at], yr.at[2, at], source)

    def hop_up(k, i):
        blk = r.at[yy, z_of(-k), i]
        push(blk, blk, zs.at[k, i], zr.at[k, i], z_up)

    def hop_dn(k, i):
        blk = r.at[yy, z_of(k), i]
        push(blk, blk, zs.at[4 + k, i], zr.at[4 + k, i], z_dn)

    def hop(k):
        for i in range(terms):
            got(r.at[yy, z_of(-k), i], zs.at[k - 1, i], zr.at[k - 1, i], z_dn)
            if k < 4:
                hop_up(k, i)
                got(r.at[yy, z_of(k), i], zs.at[3 + k, i], zr.at[3 + k, i], z_up)
            if k < 3:
                hop_dn(k, i)

    def left_products(g):
        def one(i, carry):
            s = shs[g, 0, i]
            cols = jnp.concatenate(
                [w[s + 1 + b, v] for b in range(OWN) for v in range(vecs)], axis=1
            )
            prod = jnp.dot(l[g, i], cols, preferred_element_type=jnp.float32).astype(z.dtype)
            for b in range(OWN):
                for v in range(vecs):
                    n = b * vecs + v
                    z[b, v, g * terms + i] = prod[:, n * mr : (n + 1) * mr]
            return carry

        lax.fori_loop(0, terms, one, 0)

    per_row = CORES * terms

    def first_term(d):
        return far_y(y_of(d)) * per_row

    nothing = Y * per_row
    rs[nothing] = jnp.zeros(rs.shape[1:], rs.dtype)

    def right_blocks(p, rows):
        for d in rows:
            for c in range(CORES):
                for i in range(terms):
                    rs[(d % Y) * per_row + c * terms + i] = r[y_of(d), p * CORES + c, i]

    def right_of(rows):
        tall = []
        for d in rows:
            for c in range(CORES):
                for i in range(terms):
                    s, n = shs[far_y(y_of(d)) * CORES + c, 0, i], (d % Y) * per_row + c * terms + i
                    tall.append(jnp.concatenate([rs[jnp.where(s == q - 1, n, nothing)] for q in range(3)], axis=1))
        return jnp.concatenate(tall, axis=0)

    def left_of(sigma, v, rows):
        return jnp.concatenate([z[sigma, v, first_term(d) + k] for d in rows for k in range(per_row)], axis=1)

    def right_near(p):
        rows = (0, 1, -1)
        right_blocks(p, rows)
        lhs = jnp.concatenate([left_of(sector_of(p), v, rows) for v in range(vecs)], axis=0)
        near[...] = jnp.dot(lhs, right_of(rows), preferred_element_type=jnp.float32).reshape(near.shape)

    def right_far(p):
        sigma, rows = sector_of(p), (2,)
        right_blocks(p, rows)

        def one(v, carry):
            sums = near[v] + jnp.dot(left_of(sigma, v, rows), right_of(rows), preferred_element_type=jnp.float32)
            sbuf[0, sigma, v] = sums[:, :mr].astype(sbuf.dtype)
            acc[sigma, v] = sums[:, mr : 2 * mr]
            sbuf[1, sigma, v] = sums[:, 2 * mr :].astype(sbuf.dtype)
            for q, who in ((0, s_dn), (1, s_up)):
                copy(sbuf.at[q, sigma, v], rbuf.at[q, sigma, v], os_.at[q, sigma, v], or_.at[q, sigma, v], who).start()
            return carry

        lax.fori_loop(0, vecs, one, 0)

    @pl.when(stays)
    def _():
        pltpu.make_async_copy(r_hbm, r.at[yy, zz], loc.at[OWN + 4]).wait()

    for i in range(terms):
        @pl.when(moves)
        def _(i=i):
            got(r.at[yy, zz, i], ps.at[i], pr.at[i], (from_op, from_sec))

        hop_up(0, i)
        hop_dn(0, i)
    row_send(zz)

    for d in range(1, GROUPS):
        g = lax.rem(op + d, GROUPS)
        got(shv.at[g], ss.at[GROUPS - d], sr.at[g], (g, sec))
    shift_in = pltpu.make_async_copy(shv, shs, loc.at[OWN + 5])
    shift_in.start()
    shift_in.wait()
    own_l.wait()
    for k in range(OWN + 2):
        def arrived(k=k):
            pltpu.make_async_copy(w_hbm.at[:, :, pl.ds(0, mr)], w.at[k], loc.at[k]).wait()

        if k == 0:
            pl.when(op > 0)(arrived)
        elif k == OWN + 1:
            pl.when(op < GROUPS - 1)(arrived)
        else:
            arrived()
    left_near(0)
    left_products(op)
    left_near(1)

    hop(1)
    row_send(z_of(turn))
    left_sibling(0, 2)
    left_products(group(0, 1))
    left_near(2)

    hop(2)
    row_send(order[1] * CORES)
    row_send(order[1] * CORES + 1)
    left_products(g_dn)
    row_forward(order[0])
    left_far(0)
    left_products(g_up)
    left_far(1)

    hop(3)
    row_send(order[2] * CORES)
    row_send(order[2] * CORES + 1)
    left_far(2)
    left_sibling(-1, 3)
    left_products(group(-1, 1))
    left_sibling(1, 4)
    left_products(group(1, 1))
    row_forward(order[1])

    hop(4)
    row_send(order[3] * CORES)
    row_send(order[3] * CORES + 1)
    left_products(g_far)
    left_sibling(2, 7, 8)
    left_products(group(2, 1))

    row_near(order[0])
    right_near(order[0])
    row_forward(order[2])
    row_far(order[0])
    right_far(order[0])
    row_near(order[1])
    right_near(order[1])
    row_far(order[1])
    right_far(order[1])
    row_forward(order[3])
    row_near(order[2])
    right_near(order[2])
    row_far(order[2])
    right_far(order[2])
    row_near(order[3])
    right_near(order[3])
    row_far(order[3])
    right_far(order[3])

    def total(sigma, carry):
        for v in range(vecs):
            got(rbuf.at[0, sigma, v], os_.at[0, sigma, v], or_.at[0, sigma, v], s_up)
            got(rbuf.at[1, sigma, v], os_.at[1, sigma, v], or_.at[1, sigma, v], s_dn)
        for v in range(vecs):
            above = rbuf[0, sigma, v].astype(jnp.float32)
            below = rbuf[1, sigma, v].astype(jnp.float32)
            whole = acc[sigma, v]
            whole = whole + jnp.where(jnp.full(above.shape, sec, jnp.int32) < SECTORS - 1, above, 0.0)
            whole = whole + jnp.where(jnp.full(below.shape, sec, jnp.int32) > 0, below, 0.0)
            at = pl.multiple_of(sigma * mr, mr)
            out[v, :, pl.ds(at, mr)] = whole.astype(out.dtype)
        return carry

    lax.fori_loop(0, OWN, total, 0)

    for c in sent:
        c.wait_send()

    @pl.when(moves)
    def _():
        for i in range(terms):
            copy(r_hbm.at[i], r.at[to_y, to_z, i], ps.at[i], pr.at[i], (to_op, to_sec)).wait_send()

    def drain(sigma, carry):
        for v in range(vecs):
            for q, who in ((0, s_dn), (1, s_up)):
                copy(
                    sbuf.at[q, sigma, v], rbuf.at[q, sigma, v], os_.at[q, sigma, v], or_.at[q, sigma, v], who
                ).wait_send()
        return carry

    lax.fori_loop(0, OWN, drain, 0)


def on_device(wavefunction, left_ops, right_ops, term_shift):
    ml, vecs, _ = wavefunction.shape
    terms, mr = left_ops.shape[1], right_ops.shape[2]
    every = GROUPS * terms
    flops = 2 * every * ml * ml * vecs * OWN * mr + 2 * every * vecs * ml * mr * OWN * mr
    anywhere = pl.BlockSpec(memory_space=pl.ANY)
    dma = pltpu.SemaphoreType.DMA
    bf16 = wavefunction.dtype
    result = pl.pallas_call(
        kernel,
        out_shape=jax.ShapeDtypeStruct((vecs, ml, OWN * mr), bf16),
        in_specs=[anywhere, anywhere, anywhere, pl.BlockSpec(memory_space=pltpu.SMEM)],
        out_specs=pl.BlockSpec(memory_space=pltpu.VMEM),
        scratch_shapes=[
            pltpu.VMEM((OWN + 2, vecs, ml, mr), bf16),
            pltpu.VMEM((GROUPS, terms, ml, ml), bf16),
            pltpu.VMEM((Y, Z, terms, mr, mr), bf16),
            pltpu.VMEM((OWN, vecs, every, ml, mr), bf16),
            pltpu.VMEM((every + 1, mr, mr), bf16),
            pltpu.VMEM((vecs, ml, 3 * mr), jnp.float32),
            pltpu.VMEM((OWN, vecs, ml, mr), jnp.float32),
            pltpu.VMEM((2, OWN, vecs, ml, mr), bf16),
            pltpu.VMEM((2, OWN, vecs, ml, mr), bf16),
            pltpu.VMEM((GROUPS, 8, 128), jnp.int32),
            pltpu.SMEM((GROUPS, 8, 128), jnp.int32),
            dma((OWN + 6,)),
            dma((terms,)), dma((terms,)),
            dma((7, terms)), dma((7, terms)),
            dma((3, Z)), dma((3, Z)),
            dma((9, terms)), dma((9, terms)),
            dma((GROUPS,)), dma((GROUPS,)),
            dma((2, OWN, vecs)), dma((2, OWN, vecs)),
        ],
        compiler_params=pltpu.CompilerParams(
            collective_id=0, has_side_effects=True, vmem_limit_bytes=56 * 2**20
        ),
        cost_estimate=pl.CostEstimate(flops=flops, bytes_accessed=4 * 2**20, transcendentals=0),
    )(
        jnp.transpose(wavefunction, (1, 0, 2)),
        jnp.transpose(left_ops, (1, 0, 2)),
        right_ops.reshape(terms, mr, mr),
        term_shift,
    )
    return jnp.transpose(result, (1, 0, 2))


def solution(mesh):
    in_specs = (P("sec", None, None), P("sec", "op", None), P("op", "sec", None, None), P("op"))
    out_specs = P("sec", None, "op")
    return jax.shard_map(
        on_device, mesh=mesh, in_specs=in_specs, out_specs=out_specs, check_vma=False
    )
```

```python
import jax
import jax.numpy as jnp
from jax import lax
from jax.experimental import pallas as pl
from jax.experimental.pallas import tpu as pltpu
from jax.sharding import PartitionSpec as P

X, CORES, Y, Z = 4, 2, 4, 8
GROUPS = X * CORES
SECTORS = Y * Z
OWN = SECTORS // GROUPS
EVEN = 1
MESH = pl.DeviceIdType.MESH


def kernel(
    w_hbm, l_hbm, r_hbm, sh_in, out,
    w, l, r, z, rs, near, acc, sbuf, rbuf, shv, shs,
    loc, ps, pr, zs, zr, ys, yr, ls, lr, ss, sr, os_, or_,
):
    op, sec = lax.axis_index("op"), lax.axis_index("sec")
    xx, core = lax.div(op, CORES), lax.rem(op, CORES)
    yy, zz = lax.div(sec, Z), lax.rem(sec, Z)
    vecs, ml, mr = w.shape[1], w.shape[2], w.shape[3]
    terms = l.shape[1]
    half = ml // 2

    def group(dx, other=0):
        return lax.rem(xx + dx + X, X) * CORES + (lax.rem(core + other, CORES))

    def z_of(d):
        return lax.rem(zz + d + Z, Z)

    def y_of(d):
        return lax.rem(yy + d + Y, Y)

    x_up, x_dn, sib = (group(1), sec), (group(-1), sec), (group(0, 1), sec)
    z_up, z_dn = (op, yy * Z + z_of(1)), (op, yy * Z + z_of(-1))
    y_up, y_dn = (op, y_of(1) * Z + zz), (op, y_of(-1) * Z + zz)
    s_up = (op, lax.rem(sec + 1, SECTORS))
    s_dn = (op, lax.rem(sec + SECTORS - 1, SECTORS))
    def pair_of(n, c):
        return lax.rem(n + OWN - 1 + 2 * c, OWN)

    def sector_of(p):
        return lax.rem(p + 1 + 2 * core, OWN)

    def far_y(d):
        return lax.rem(d + 2, Y)

    to_op = lax.div(sec, OWN)
    to_y, to_z = far_y(xx), pair_of(lax.rem(sec, OWN), lax.rem(to_op, CORES)) * CORES + core
    to_sec = to_y * Z + to_z
    from_op = far_y(yy) * CORES + lax.rem(zz, CORES)
    from_sec = op * OWN + sector_of(lax.div(zz, CORES))
    stays = (to_op == op) & (to_sec == sec)
    moves = jnp.logical_not(stays)

    first = op * OWN - 1
    for k in range(OWN + 2):
        def load(k=k):
            at = pl.multiple_of((first + k) * mr, mr)
            pltpu.make_async_copy(w_hbm.at[:, :, pl.ds(at, mr)], w.at[k], loc.at[k]).start()

        def blank(k=k):
            w[k] = jnp.zeros(w.shape[1:], w.dtype)

        if k == 0:
            pl.when(op > 0)(load)
            pl.when(op == 0)(blank)
        elif k == OWN + 1:
            pl.when(op < GROUPS - 1)(load)
            pl.when(op == GROUPS - 1)(blank)
        else:
            load()
    own_l = pltpu.make_async_copy(l_hbm, l.at[op], loc.at[OWN + 2])
    own_l.start()
    lane = lax.broadcasted_iota(jnp.int32, shv.shape[1:], 1)
    own_shifts = jnp.zeros(shv.shape[1:], jnp.int32)
    for i in range(terms):
        own_shifts = jnp.where(lane == i, jnp.full(lane.shape, sh_in[i], jnp.int32), own_shifts)
    shv[op] = own_shifts

    for q, end in ((0, SECTORS - 1), (1, 0)):
        @pl.when(sec == end)
        def _(q=q):
            rbuf[q] = jnp.zeros(rbuf.shape[1:], rbuf.dtype)

    barrier = pltpu.get_barrier_semaphore()
    greet = [z_up, z_dn, y_up, y_dn, s_up, s_dn]
    greet += [(lax.rem(op + d, GROUPS), sec) for d in range(1, GROUPS)]
    for who in greet:
        pl.semaphore_signal(barrier, inc=1, device_id=who, device_id_type=MESH)

    @pl.when(moves)
    def _():
        for who in ((to_op, to_sec), (from_op, from_sec)):
            pl.semaphore_signal(barrier, inc=1, device_id=who, device_id_type=MESH)
        pl.semaphore_wait(barrier, len(greet) + 2)

    @pl.when(stays)
    def _():
        pl.semaphore_wait(barrier, len(greet))

    turn = 1 - 2 * lax.rem(zz, 2)
    s0 = lax.div(zz, CORES)
    order = [s0, lax.rem(s0 - turn + OWN, OWN), lax.rem(s0 + turn + OWN, OWN), lax.rem(s0 + 2, OWN)]

    sent = []

    def copy(src, dst, send, recv, who):
        return pltpu.make_async_remote_copy(
            src_ref=src, dst_ref=dst, send_sem=send, recv_sem=recv, device_id=who, device_id_type=MESH
        )

    def push(src, dst, send, recv, who):
        c = copy(src, dst, send, recv, who)
        c.start()
        sent.append(c)

    def got(dst, send, recv, who):
        copy(dst, dst, send, recv, who).wait_recv()

    @pl.when(moves)
    def _():
        for i in range(terms):
            copy(r_hbm.at[i], r.at[to_y, to_z, i], ps.at[i], pr.at[i], (to_op, to_sec)).start()

    @pl.when(stays)
    def _():
        pltpu.make_async_copy(r_hbm, r.at[yy, zz], loc.at[OWN + 4]).start()

    for d in range(1, GROUPS):
        push(shv.at[op], shv.at[op], ss.at[d], sr.at[op], (lax.rem(op + d, GROUPS), sec))
    for i in range(terms):
        push(l_hbm.at[i], l.at[op, i], ls.at[0, i], lr.at[0, i], x_up)
        push(l_hbm.at[i], l.at[op, i], ls.at[1, i], lr.at[1, i], x_dn)
        push(l_hbm.at[i], l.at[op, i], ls.at[2, i], lr.at[2, i], sib)
    g_dn, g_up, g_far = group(-1), group(1), group(2)

    def left_near(i):
        blk, part = l.at[g_dn, i], l.at[g_dn, i, :half]
        got(blk, ls.at[0, i], lr.at[0, i], x_dn)
        push(part, part, ls.at[5, i], lr.at[5, i], x_up)
        push(blk, blk, ls.at[3, i], lr.at[3, i], sib)
        blk, part = l.at[g_up, i], l.at[g_up, i, half:]
        got(blk, ls.at[1, i], lr.at[1, i], x_up)
        push(part, part, ls.at[6, i], lr.at[6, i], x_dn)
        push(blk, blk, ls.at[4, i], lr.at[4, i], sib)

    def left_far(i):
        part = l.at[g_far, i, :half]
        got(part, ls.at[5, i], lr.at[5, i], x_dn)
        push(part, part, ls.at[7, i], lr.at[7, i], sib)
        part = l.at[g_far, i, half:]
        got(part, ls.at[6, i], lr.at[6, i], x_up)
        push(part, part, ls.at[8, i], lr.at[8, i], sib)

    def left_sibling(dx, *ways):
        for i in range(terms):
            for way in ways:
                blk = l.at[group(dx, 1), i]
                if len(ways) > 1:
                    blk = l.at[group(dx, 1), i, :half] if way == ways[0] else l.at[group(dx, 1), i, half:]
                got(blk, ls.at[way, i], lr.at[way, i], sib)

    def row_send(c):
        blk = r.at[yy, c]
        push(blk, blk, ys.at[0, c], yr.at[0, c], y_up)
        push(blk, blk, ys.at[1, c], yr.at[1, c], y_dn)

    def passage(c, p):
        late = sum((p == order[k]).astype(jnp.int32) for k in range(EVEN, OWN)) > 0
        if c:
            upward = jnp.where((zz == Z - 1) & late, 1, 0)
        else:
            upward = jnp.where((zz == 0) & late, 0, 1)
        to = (op, y_of(2 * upward - 1) * Z + zz)
        source = (op, y_of(1 - 2 * upward) * Z + zz)
        return 1 - upward, to, source

    def row_forward(p):
        for c in range(CORES):
            at = p * CORES + c
            way, to, source = passage(c, p)
            blk = r.at[y_of(2 * way - 1), at]
            got(blk, ys.at[way, at], yr.at[way, at], source)
            push(blk, blk, ys.at[2, at], yr.at[2, at], to)

    def row_near(p):
        for c in range(CORES):
            at = p * CORES + c
            way, to, _ = passage(c, p)
            got(r.at[y_of(1 - 2 * way), at], ys.at[1 - way, at], yr.at[1 - way, at], to)

    def row_far(p):
        for c in range(CORES):
            at = p * CORES + c
            _, _, source = passage(c, p)
            got(r.at[y_of(2), at], ys.at[2, at], yr.at[2, at], source)

    def hop_up(k, i):
        blk = r.at[yy, z_of(-k), i]
        push(blk, blk, zs.at[k, i], zr.at[k, i], z_up)

    def hop_dn(k, i):
        blk = r.at[yy, z_of(k), i]
        push(blk, blk, zs.at[4 + k, i], zr.at[4 + k, i], z_dn)

    def hop(k):
        for i in range(terms):
            got(r.at[yy, z_of(-k), i], zs.at[k - 1, i], zr.at[k - 1, i], z_dn)
            if k < 4:
                hop_up(k, i)
                got(r.at[yy, z_of(k), i], zs.at[3 + k, i], zr.at[3 + k, i], z_up)
            if k < 3:
                hop_dn(k, i)

    def left_products(g):
        def one(i, carry):
            s = shs[g, 0, i]
            cols = jnp.concatenate(
                [w[s + 1 + b, v] for b in range(OWN) for v in range(vecs)], axis=1
            )
            prod = jnp.dot(l[g, i], cols, preferred_element_type=jnp.float32).astype(z.dtype)
            for b in range(OWN):
                for v in range(vecs):
                    n = b * vecs + v
                    z[b, v, g * terms + i] = prod[:, n * mr : (n + 1) * mr]
            return carry

        lax.fori_loop(0, terms, one, 0)

    has = (sec > 0, sec < SECTORS - 1)

    def shift_copy(q, sigma, v):
        return copy(
            sbuf.at[q, sigma, v], rbuf.at[q, sigma, v], os_.at[q, sigma, v], or_.at[q, sigma, v], (s_dn, s_up)[q]
        )

    per_row = CORES * terms

    def first_term(d):
        return far_y(y_of(d)) * per_row

    nothing = Y * per_row
    rs[nothing] = jnp.zeros(rs.shape[1:], rs.dtype)

    def right_blocks(p, rows):
        for d in rows:
            for c in range(CORES):
                for i in range(terms):
                    rs[(d % Y) * per_row + c * terms + i] = r[y_of(d), p * CORES + c, i]

    def right_of(rows):
        tall = []
        for d in rows:
            for c in range(CORES):
                for i in range(terms):
                    s, n = shs[far_y(y_of(d)) * CORES + c, 0, i], (d % Y) * per_row + c * terms + i
                    tall.append(jnp.concatenate([rs[jnp.where(s == q - 1, n, nothing)] for q in range(3)], axis=1))
        return jnp.concatenate(tall, axis=0)

    def left_of(sigma, v, rows):
        return jnp.concatenate([z[sigma, v, first_term(d) + k] for d in rows for k in range(per_row)], axis=1)

    def right_near(p):
        rows = (0, 1, -1)
        right_blocks(p, rows)
        lhs = jnp.concatenate([left_of(sector_of(p), v, rows) for v in range(vecs)], axis=0)
        near[...] = jnp.dot(lhs, right_of(rows), preferred_element_type=jnp.float32).reshape(near.shape)

    def right_far(p):
        sigma, rows = sector_of(p), (2,)
        right_blocks(p, rows)

        def one(v, carry):
            sums = near[v] + jnp.dot(left_of(sigma, v, rows), right_of(rows), preferred_element_type=jnp.float32)
            sbuf[0, sigma, v] = sums[:, :mr].astype(sbuf.dtype)
            acc[sigma, v] = sums[:, mr : 2 * mr]
            sbuf[1, sigma, v] = sums[:, 2 * mr :].astype(sbuf.dtype)
            for q in range(2):
                pl.when(has[q])(lambda q=q: shift_copy(q, sigma, v).start())
            return carry

        lax.fori_loop(0, vecs, one, 0)

    @pl.when(stays)
    def _():
        pltpu.make_async_copy(r_hbm, r.at[yy, zz], loc.at[OWN + 4]).wait()

    for i in range(terms):
        @pl.when(moves)
        def _(i=i):
            got(r.at[yy, zz, i], ps.at[i], pr.at[i], (from_op, from_sec))

        hop_up(0, i)
        hop_dn(0, i)
    row_send(zz)

    for d in range(1, GROUPS):
        g = lax.rem(op + d, GROUPS)
        got(shv.at[g], ss.at[GROUPS - d], sr.at[g], (g, sec))
    shift_in = pltpu.make_async_copy(shv, shs, loc.at[OWN + 5])
    shift_in.start()
    shift_in.wait()
    own_l.wait()
    for k in range(OWN + 2):
        def arrived(k=k):
            pltpu.make_async_copy(w_hbm.at[:, :, pl.ds(0, mr)], w.at[k], loc.at[k]).wait()

        if k == 0:
            pl.when(op > 0)(arrived)
        elif k == OWN + 1:
            pl.when(op < GROUPS - 1)(arrived)
        else:
            arrived()
    left_near(0)
    left_products(op)
    left_near(1)

    hop(1)
    row_send(z_of(turn))
    left_sibling(0, 2)
    left_products(group(0, 1))
    left_near(2)

    hop(2)
    row_send(order[1] * CORES)
    row_send(order[1] * CORES + 1)
    left_products(g_dn)
    row_forward(order[0])
    left_far(0)
    left_products(g_up)
    left_far(1)

    hop(3)
    row_send(order[2] * CORES)
    row_send(order[2] * CORES + 1)
    left_far(2)
    left_sibling(-1, 3)
    left_products(group(-1, 1))
    left_sibling(1, 4)
    left_products(group(1, 1))
    row_forward(order[1])

    hop(4)
    row_send(order[3] * CORES)
    row_send(order[3] * CORES + 1)
    left_products(g_far)
    left_sibling(2, 7, 8)
    left_products(group(2, 1))

    row_near(order[0])
    right_near(order[0])
    row_forward(order[2])
    row_far(order[0])
    right_far(order[0])
    row_near(order[1])
    right_near(order[1])
    row_far(order[1])
    right_far(order[1])
    row_forward(order[3])
    row_near(order[2])
    right_near(order[2])
    row_far(order[2])
    right_far(order[2])
    row_near(order[3])
    right_near(order[3])
    row_far(order[3])
    right_far(order[3])

    for c in sent:
        c.wait_send()

    @pl.when(moves)
    def _():
        for i in range(terms):
            copy(r_hbm.at[i], r.at[to_y, to_z, i], ps.at[i], pr.at[i], (to_op, to_sec)).wait_send()

    def drain(sigma, carry):
        for v in range(vecs):
            for q in range(2):
                pl.when(has[q])(lambda q=q, v=v: shift_copy(q, sigma, v).wait_send())
        return carry

    for p in order[:3]:
        drain(sector_of(p), 0)

    def total(sigma, carry):
        for v in range(vecs):
            for q in range(2):
                pl.when(has[1 - q])(lambda q=q, v=v: shift_copy(q, sigma, v).wait_recv())
        for v in range(vecs):
            whole = acc[sigma, v] + rbuf[0, sigma, v].astype(jnp.float32) + rbuf[1, sigma, v].astype(jnp.float32)
            at = pl.multiple_of(sigma * mr, mr)
            out[v, :, pl.ds(at, mr)] = whole.astype(out.dtype)
        return carry

    lax.fori_loop(0, OWN, total, 0)

    drain(sector_of(order[3]), 0)


def on_device(wavefunction, left_ops, right_ops, term_shift):
    ml, vecs, _ = wavefunction.shape
    terms, mr = left_ops.shape[1], right_ops.shape[2]
    every = GROUPS * terms
    flops = 2 * every * ml * ml * vecs * OWN * mr + 2 * every * vecs * ml * mr * OWN * mr
    anywhere = pl.BlockSpec(memory_space=pl.ANY)
    dma = pltpu.SemaphoreType.DMA
    bf16 = wavefunction.dtype
    result = pl.pallas_call(
        kernel,
        out_shape=jax.ShapeDtypeStruct((vecs, ml, OWN * mr), bf16),
        in_specs=[anywhere, anywhere, anywhere, pl.BlockSpec(memory_space=pltpu.SMEM)],
        out_specs=pl.BlockSpec(memory_space=pltpu.VMEM),
        scratch_shapes=[
            pltpu.VMEM((OWN + 2, vecs, ml, mr), bf16),
            pltpu.VMEM((GROUPS, terms, ml, ml), bf16),
            pltpu.VMEM((Y, Z, terms, mr, mr), bf16),
            pltpu.VMEM((OWN, vecs, every, ml, mr), bf16),
            pltpu.VMEM((every + 1, mr, mr), bf16),
            pltpu.VMEM((vecs, ml, 3 * mr), jnp.float32),
            pltpu.VMEM((OWN, vecs, ml, mr), jnp.float32),
            pltpu.VMEM((2, OWN, vecs, ml, mr), bf16),
            pltpu.VMEM((2, OWN, vecs, ml, mr), bf16),
            pltpu.VMEM((GROUPS, 8, 128), jnp.int32),
            pltpu.SMEM((GROUPS, 8, 128), jnp.int32),
            dma((OWN + 6,)),
            dma((terms,)), dma((terms,)),
            dma((7, terms)), dma((7, terms)),
            dma((3, Z)), dma((3, Z)),
            dma((9, terms)), dma((9, terms)),
            dma((GROUPS,)), dma((GROUPS,)),
            dma((2, OWN, vecs)), dma((2, OWN, vecs)),
        ],
        compiler_params=pltpu.CompilerParams(
            collective_id=0, has_side_effects=True, vmem_limit_bytes=56 * 2**20
        ),
        cost_estimate=pl.CostEstimate(flops=flops, bytes_accessed=4 * 2**20, transcendentals=0),
    )(
        jnp.transpose(wavefunction, (1, 0, 2)),
        jnp.transpose(left_ops, (1, 0, 2)),
        right_ops.reshape(terms, mr, mr),
        term_shift,
    )
    return jnp.transpose(result, (1, 0, 2))


def solution(mesh):
    in_specs = (P("sec", None, None), P("sec", "op", None), P("op", "sec", None, None), P("op"))
    out_specs = P("sec", None, "op")
    return jax.shard_map(
        on_device, mesh=mesh, in_specs=in_specs, out_specs=out_specs, check_vma=False
    )
```
